32 devices in a mesh: section: 4 (over y, x), tile: 8 (over z, core).
Axes of the slice: x: 2, y: 2, z: 4, core: 2. Of those that a mesh axis runs over, the one named last changes fastest.
Arguments:
- forcing: bfloat16 [262144, 128], P(('section', 'tile')), may hold values from -6 to 6
- w_in: bfloat16 [128, 1024], replicated, may hold values from -0.5 to 0.5
- bias_in: float32 [1024], replicated, may hold values from -3 to 3
- w_out: bfloat16 [1024, 128], replicated, may hold values from -0.1875 to 0.1875
- target_tile_index: int32 [262144, 1], P(('section', 'tile')), may hold values from 0 to 7; in each aligned block of 8192 rows (0 to 8191, 8192 to 16383, ...) at most 2048 rows name the same one
- reach_slot: int32 [262144], P(('section', 'tile')), may hold values from 0 to 63
- k_ratio: float32 [4, 512], P(None, ('section', 'tile')), may hold values from 1 to 40
- x_weight: float32 [4, 512], P(None, ('section', 'tile')), may hold values from 0.05 to 0.3
- down_link: int32 [4, 512], P(None, ('section', 'tile')), may hold values from 0 to 127
- cotangent: float32 [4, 512, 128], P(None, ('section', 'tile')), may hold values from -6 to 6
Outputs:
- discharge: float32 [4, 512, 128], P(None, ('section', 'tile'))
- grad_w_in: float32 [128, 1024], replicated
- grad_bias: float32 [1024], replicated
- grad_w_out: float32 [1024, 128], replicated
The draws below stay inside these ranges and needn't reach their ends.
Inputs may be any that keep to these rules, and one draw needn't show every extreme that they name: `target_tile_index`: among the catchments of one device, at most 2048 name the same tile, a bound that some block reaches. `down_link`: entries of last-section reaches are not used.
All inputs are finite; a program needn't handle non-finite values.
Results may differ from the reference program's by a relative error of at most 0.0038.
Values may be sent and summed in bfloat16 or wider, within the bound.
A program may use at most 192 MiB of HBM per device.

```python
import math
import jax
import jax.numpy as jnp
import numpy as np
from jax import lax

FEAT = 128
HID = 1024
STEPS = 128
G = 4
CELLS = 8192
R_DEV = 16
CAP = 2048
CATCH = 262144
REACHES = 512
DOWN_SPAN = 128
N_SECTION = 4
N_TILE = 8


def place_ends(result, rng, least, largest):
    longest = result.shape.index(max(result.shape))
    spots = []
    for shift in (0, 1):
        where = [jax.random.randint(jax.random.fold_in(rng, axis), (), 0, length) for axis, length in enumerate(result.shape)]
        where[longest] = (where[longest] + shift) % result.shape[longest]
        spots.append(tuple(where))
    return result.at[spots[0]].set(least).at[spots[1]].set(largest)


def levels(stream_key, shape, shards, smallest, high):
    def one(position, blocks):
        heights = jax.random.uniform(jax.random.fold_in(jax.random.fold_in(stream_key, 6), position), (blocks,), jnp.float32, smallest / len(shards), high / len(shards))
        return jnp.repeat(jnp.exp(heights), shape[position] // blocks).reshape((-1,) + (1,) * (len(shape) - position - 1))

    factor_of = one(*shards[0])
    for cut in shards[1:]:
        factor_of = factor_of * one(*cut)
    return factor_of


def deal_out(own_key, own, number, rows, count, top, most, skew):
    order = jax.random.permutation(own_key, count)
    crowded, ordinary = shares(count, rows * top, most, skew, True), shares(count, rows * top, most, skew, False)
    places = jnp.arange(count)

    def named(sizes, offset_by):
        used = int((sizes > 0).sum())
        fixed = max(1, used // 4)
        shifted = fixed + (places - fixed + offset_by * (used - fixed)) % max(1, count - fixed)
        return jnp.zeros((count,), jnp.int32).at[order[jnp.where(places < fixed, places, shifted)]].set(jnp.asarray(sizes, jnp.int32))

    sizes = jnp.where(number % 4 == 0, named(crowded, number // 4), named(ordinary, number - number // 4 - 1))
    mixed = jax.random.permutation(jax.random.fold_in(own, 3), count)
    source_of, receiver = mixed[0:count // 2 * 2:2], mixed[1:count // 2 * 2:2]
    slack = jnp.minimum(sizes[source_of] - 1, most - sizes[receiver]) // 2
    slack = jnp.where((source_of == order[0]) | (receiver == order[0]) | (sizes[receiver] == 0), 0, jnp.maximum(slack, 0))
    shifted = jax.random.randint(jax.random.fold_in(own, 4), (count // 2,), 0, 1 << 20) % (slack + 1)
    sizes = sizes.at[source_of].add(-shifted).at[receiver].add(shifted)
    members = jnp.searchsorted(jnp.cumsum(sizes), jnp.arange(rows * top), side="right").astype(jnp.int32)
    table = members.reshape(top, rows).T
    table = table[jax.random.permutation(jax.random.fold_in(own, 1), rows)]
    offset_by = jax.random.randint(jax.random.fold_in(own, 2), (rows, 1), 0, top)
    return jnp.take_along_axis(table, (jnp.arange(top)[None, :] + offset_by) % top, axis=1)


def shares(number_of, total, reach, slope, full):
    portions = [(1 << 20) // math.isqrt(grade ** slope) + 1 for grade in range(1, number_of + 1)]
    largest = reach if full else min(reach, max(-(-total // number_of), total * portions[0] // sum(portions)))
    least = 1 if total - largest >= number_of - 1 else 0
    holding, spare = [largest] + [least] * (number_of - 1), total - largest - least * (number_of - 1)
    while spare > 0:
        movable = [i for i in range(1, number_of) if holding[i] < largest] or [i for i in range(1, number_of) if holding[i] < reach]
        pool, left = sum([portions[i] for i in movable]), spare
        for i in movable:
            extra = min(reach - holding[i], max(1, left * portions[i] // pool), spare)
            holding[i] = holding[i] + extra
            spare = spare - extra
    return np.array(holding)


def gaussian(rng, dims, spread, reach, pieces=(), held_as=jnp.bfloat16):
    result = spread * jax.random.normal(rng, dims, jnp.float32)
    if pieces:
        result = result * levels(rng, dims, pieces, -0.22, 0.18)
    return jnp.clip(result, -reach, reach).astype(held_as)


def setup_inputs(seed: int = 0) -> dict:
    streams_of = jax.random.split(jax.random.key(seed), 11)
    forcing = gaussian(streams_of[0], (CATCH, FEAT), 1.0, 6.0, ((0, 32),))
    w_in = gaussian(streams_of[1], (FEAT, HID), FEAT ** -0.5, 0.5)
    bias_in = gaussian(streams_of[2], (HID,), 0.5, 3.0, (), jnp.float32)
    w_out = gaussian(streams_of[3], (HID, STEPS), HID ** -0.5, 0.1875)
    target_tile_index_keys = jax.random.split(jax.random.fold_in(streams_of[4], 1), CATCH // CELLS)
    target_tile_index_turns = jax.random.permutation(jax.random.fold_in(streams_of[4], 3), CATCH // CELLS)
    target_tile_index = jax.vmap(lambda own, number: deal_out(jax.random.fold_in(streams_of[4], 2), own, number, CELLS, N_TILE, 1, CAP, 2))(target_tile_index_keys, target_tile_index_turns).reshape((CATCH, 1))
    reach_slot = place_ends(jax.random.randint(streams_of[5], (CATCH,), 0, G * R_DEV), jax.random.fold_in(streams_of[5], 1), 0, (G * R_DEV) - 1).astype(jnp.int32)
    k_ratio = jnp.clip(jnp.exp(math.log(40.0) - 3.6888795 * jax.random.uniform(streams_of[6], (G, REACHES), jnp.float32) ** levels(streams_of[6], (G, REACHES), ((1, 32),), -0.2, 0.2)), 1.0, 40.0)
    x_weight = jnp.clip(0.05 + 0.25 * jax.random.uniform(streams_of[7], (G, REACHES), jnp.float32) ** levels(streams_of[7], (G, REACHES), ((1, 32),), -0.2, 0.2), 0.05, 0.3)
    down_link = place_ends(jax.random.randint(streams_of[8], (G, REACHES), 0, DOWN_SPAN), jax.random.fold_in(streams_of[8], 1), 0, DOWN_SPAN - 1).astype(jnp.int32)
    cotangent = gaussian(streams_of[9], (G, REACHES, STEPS), 1.0, 6.0, ((1, 32),), jnp.float32)
    return dict(forcing=forcing, w_in=w_in, bias_in=bias_in, w_out=w_out, target_tile_index=target_tile_index, reach_slot=reach_slot, k_ratio=k_ratio, x_weight=x_weight, down_link=down_link, cotangent=cotangent)


def coefficients(k_ratio, x_weight):
    storage = 2.0 * k_ratio * (1.0 - x_weight)
    denom = storage + 1.0
    c_now = (1.0 - 2.0 * k_ratio * x_weight) / denom
    c_prev = (1.0 + 2.0 * k_ratio * x_weight) / denom
    c_keep = (storage - 1.0) / denom
    c_side = 2.0 / denom
    return (c_now, c_prev, c_keep, c_side)

def route(inflow, lateral, c_now, c_prev, c_keep, c_side):
    before = jnp.concatenate([jnp.zeros_like(inflow[:, :1]), inflow[:, :-1]], axis=1)
    drive = c_now[:, None] * inflow + c_prev[:, None] * before + c_side[:, None] * lateral

    def advance(state, column):
        state = c_keep * state + column
        return (state, state)
    _, outs = lax.scan(advance, jnp.zeros_like(c_keep), drive.T)
    return outs.T

def reference(forcing, w_in, bias_in, w_out, target_tile_index, reach_slot, k_ratio, x_weight, down_link, cotangent):
    pre = jnp.dot(forcing, w_in, preferred_element_type=jnp.float32) + bias_in
    hidden = jax.nn.silu(pre).astype(jnp.bfloat16)
    runoff = (0.125 * jnp.dot(hidden, w_out, preferred_element_type=jnp.float32)).astype(jnp.bfloat16)
    span = N_TILE * R_DEV
    source = jnp.arange(CATCH, dtype=jnp.int32) // CELLS
    section_of = source // N_TILE
    group_of = reach_slot // R_DEV
    inside_section = reach_slot % R_DEV
    target = group_of * REACHES + section_of * span + target_tile_index[:, 0] * R_DEV + inside_section
    lateral = jax.ops.segment_sum(runoff.astype(jnp.float32), target, G * REACHES)
    lateral = lateral.reshape(G, N_SECTION, span, STEPS)
    c_now, c_prev, c_keep, c_side = [c.reshape(G, N_SECTION, span) for c in coefficients(k_ratio, x_weight)]
    links = down_link.reshape(G, N_SECTION, span)

    def network(lat):
        outs = []
        inflow = jnp.zeros((G, span, STEPS), jnp.float32)
        for section in range(N_SECTION):
            flow = jax.vmap(route)(inflow, lat[:, section], c_now[:, section], c_prev[:, section], c_keep[:, section], c_side[:, section])
            outs.append(flow)
            inflow = jax.vmap(lambda q, d: jax.ops.segment_sum(q, d, span))(flow, links[:, section])
        return jnp.stack(outs, axis=1)
    discharge, pullback = jax.vjp(network, lateral)
    glat, = pullback(cotangent.reshape(G, N_SECTION, span, STEPS))
    grad_runoff = jnp.take(glat.reshape(G * REACHES, STEPS), target, axis=0).astype(jnp.bfloat16)
    grad_w_out = 0.125 * jnp.dot(hidden.T, grad_runoff, preferred_element_type=jnp.float32)
    grad_hidden = 0.125 * jnp.dot(grad_runoff, w_out.T, preferred_element_type=jnp.float32)
    sig = jax.nn.sigmoid(pre)
    grad_pre = grad_hidden * sig * (1.0 + pre * (1.0 - sig))
    grad_bias = lax.optimization_barrier(jnp.sum(grad_pre, axis=0))
    grad_w_in = jnp.dot(forcing.T, grad_pre.astype(jnp.bfloat16), preferred_element_type=jnp.float32)
    return (discharge.reshape(G, REACHES, STEPS), grad_w_in, grad_bias, grad_w_out)
```

```python
import functools

import jax
import jax.numpy as jnp
from jax import lax
from jax.experimental import pallas as pl
from jax.experimental.pallas import tpu as pltpu
from jax.sharding import PartitionSpec as P

F32 = jnp.float32
BF16 = jnp.bfloat16


def coefficients(k_ratio, x_weight):
    storage = 2.0 * k_ratio * (1.0 - x_weight)
    denom = storage + 1.0
    c_now = (1.0 - 2.0 * k_ratio * x_weight) / denom
    c_prev = (1.0 + 2.0 * k_ratio * x_weight) / denom
    c_keep = (storage - 1.0) / denom
    c_side = 2.0 / denom
    return (c_now, c_prev, c_keep, c_side)


def later(x, n):
    t = lax.broadcasted_iota(jnp.int32, x.shape, 0)
    return jnp.where(t >= n, pltpu.roll(x, n, 0), 0.0)


def earlier(x, n):
    t = lax.broadcasted_iota(jnp.int32, x.shape, 0)
    return jnp.where(t < x.shape[0] - n, pltpu.roll(x, x.shape[0] - n, 0), 0.0)


def scan_time(drive, decay, shift):
    n = 1
    while n < drive.shape[0]:
        drive = drive + decay * shift(drive, n)
        decay = decay * decay
        n *= 2
    return drive


def exact_dot(x, table, dims):
    total = None
    for _ in range(3):
        part = x.astype(BF16)
        x = x - part.astype(F32)
        term = lax.dot_general(part, table, (dims, ((), ())), preferred_element_type=F32)
        total = term if total is None else total + term
    return total


def section_row(params, first, groups, lanes):
    return jnp.concatenate([params[first + g : first + g + 1, lanes] for g in range(groups)], axis=1)


def section_coefs(params, groups, lanes):
    return coefficients(
        section_row(params, 0, groups, lanes), section_row(params, groups, groups, lanes)
    )


def link_table(params, g, groups, lanes, span):
    links = params[2 * groups + g : 2 * groups + g + 1, lanes]
    rows = lax.broadcasted_iota(jnp.int32, (span, span), 0).astype(F32)
    return (rows == links).astype(BF16)


def adjoint_chain(params, cot, groups, sections, span, emit):
    extra = None
    for s in reversed(range(sections)):
        lanes = slice(s * span, (s + 1) * span)
        c_now, c_prev, c_keep, c_side = section_coefs(params, groups, lanes)
        grad = jnp.concatenate([cot(g, s).T for g in range(groups)], axis=1)
        if extra is not None:
            grad = grad + extra
        adj = scan_time(grad, c_keep, earlier)
        emit(s, c_side * adj)
        if s > 0:
            grad_in = c_now * adj + c_prev * earlier(adj, 1)
            up = slice((s - 1) * span, s * span)
            extra = jnp.concatenate(
                [
                    exact_dot(
                        grad_in[:, g * span : (g + 1) * span],
                        link_table(params, g, groups, up, span),
                        ((1,), (0,)),
                    )
                    for g in range(groups)
                ],
                axis=1,
            )


def forward_chain(params, lat, groups, sections, span, emit):
    inflow = None
    for s in range(sections):
        lanes = slice(s * span, (s + 1) * span)
        c_now, c_prev, c_keep, c_side = section_coefs(params, groups, lanes)
        drive = c_side * jnp.concatenate([lat(g, s).T for g in range(groups)], axis=1)
        if inflow is not None:
            drive = drive + c_now * inflow + c_prev * later(inflow, 1)
        flow = scan_time(drive, c_keep, later)
        emit(s, flow)
        if s + 1 < sections:
            inflow = jnp.concatenate(
                [
                    exact_dot(
                        flow[:, g * span : (g + 1) * span],
                        link_table(params, g, groups, lanes, span),
                        ((1,), (1,)),
                    )
                    for g in range(groups)
                ],
                axis=1,
            )


def adjoint_kernel(groups, sections, span, params_ref, cot_ref, glat_ref):
    mine = lax.axis_index("section")

    def emit(s, glat):
        @pl.when(mine == s)
        def _():
            glat_ref[...] = 0.125 * glat.astype(BF16)

    adjoint_chain(
        params_ref[...],
        lambda g, s: cot_ref[g, s * span : (s + 1) * span, :],
        groups, sections, span, emit,
    )


def forward_kernel(groups, sections, span, params_ref, lat_ref, out_ref, flow_ref):
    mine = lax.axis_index("section")
    reaches = out_ref.shape[1]

    def emit(s, flow):
        @pl.when(mine == s)
        def _():
            for g in range(groups):
                flow_ref[g] = flow[:, g * span : (g + 1) * span].T

    forward_chain(
        params_ref[...],
        lambda g, s: lat_ref[g, s * span : (s + 1) * span, :],
        groups, sections, span, emit,
    )
    first = pl.multiple_of(lax.axis_index("tile") * reaches, 8)
    for g in range(groups):
        out_ref[g] = flow_ref[g, pl.ds(first, reaches), :]


def cells_kernel(x_ref, key_ref, w_in_ref, bias_ref, w_out_ref, glat_ref, grads_ref, lat_ref):
    feat, hid = w_in_ref.shape
    steps = w_out_ref.shape[1]
    cells = x_ref.shape[0]

    @pl.when(pl.program_id(0) == 0)
    def _():
        grads_ref[...] = jnp.zeros_like(grads_ref)
        lat_ref[...] = jnp.zeros_like(lat_ref)

    x = x_ref[...]
    pre = jnp.dot(x, w_in_ref[...], preferred_element_type=F32) + bias_ref[...]
    sig = 0.5 * jnp.tanh(0.5 * pre) + 0.5
    act = pre * sig
    slope = sig + act * (1.0 - sig)
    hidden = act.astype(BF16)
    runoff = (0.125 * jnp.dot(hidden, w_out_ref[...], preferred_element_type=F32)).astype(BF16)
    rows = lax.broadcasted_iota(jnp.int32, (lat_ref.shape[0], cells), 0)
    onehot = (rows == key_ref[...]).astype(F32).astype(BF16)
    lat_ref[...] += jnp.dot(onehot, runoff, preferred_element_type=F32)
    back = jnp.dot(glat_ref[...], onehot, preferred_element_type=F32)
    back_t = back.T.astype(BF16)
    back = back.astype(BF16)
    grads_ref[feat : feat + steps, :] += jnp.dot(back, hidden, preferred_element_type=F32)
    grad_hidden = lax.dot_general(
        back_t, w_out_ref[...], (((1,), (1,)), ((), ())), preferred_element_type=F32
    )
    grad_pre = grad_hidden * slope
    grads_ref[feat + steps : feat + steps + 1, :] += jnp.sum(grad_pre, axis=0, keepdims=True)
    grads_ref[0:feat, :] += jnp.dot(x.T, grad_pre.astype(BF16), preferred_element_type=F32)


def local(
    forcing, w_in, bias_in, w_out, target_tile_index, reach_slot,
    k_ratio, x_weight, down_link, cotangent,
):
    tiles = lax.axis_size("tile")
    sections = lax.axis_size("section")
    cells, feat = forcing.shape
    hid, steps = w_out.shape
    groups, reaches = k_ratio.shape
    span = tiles * reaches
    both = ("section", "tile")
    big = pltpu.CompilerParams(vmem_limit_bytes=56 << 20)

    own = jnp.concatenate([k_ratio, x_weight, down_link.astype(F32)], axis=0)
    params = lax.all_gather(own, both, axis=1, tiled=True)
    cot = lax.all_gather(cotangent, both, axis=1, tiled=True)
    glat = pl.pallas_call(
        functools.partial(adjoint_kernel, groups, sections, span),
        out_shape=jax.ShapeDtypeStruct((steps, groups * span), BF16),
        compiler_params=big,
    )(params, cot)

    key = (reach_slot // reaches) * span + target_tile_index[:, 0] * reaches + reach_slot % reaches
    block = min(cells, 1024)
    whole = lambda shape: pl.BlockSpec(shape, lambda i: (0, 0))
    grads, lateral = pl.pallas_call(
        cells_kernel,
        grid=(cells // block,),
        in_specs=[
            pl.BlockSpec((block, feat), lambda i: (i, 0)),
            pl.BlockSpec((1, block), lambda i: (0, i)),
            whole((feat, hid)), whole((1, hid)), whole((hid, steps)), whole((steps, groups * span)),
        ],
        out_specs=[whole((feat + steps + 8, hid)), whole((groups * span, steps))],
        out_shape=[
            jax.ShapeDtypeStruct((feat + steps + 8, hid), F32),
            jax.ShapeDtypeStruct((groups * span, steps), F32),
        ],
        compiler_params=big,
    )(forcing, key[None, :], w_in, bias_in[None, :], w_out, glat)

    lateral = lax.psum(lateral, "tile").reshape(groups, span, steps)
    lateral = lax.all_gather(lateral, "section", axis=1, tiled=True)
    discharge = pl.pallas_call(
        functools.partial(forward_kernel, groups, sections, span),
        out_shape=jax.ShapeDtypeStruct((groups, reaches, steps), F32),
        scratch_shapes=[pltpu.VMEM((groups, span, steps), F32)],
        compiler_params=big,
    )(params, lateral)
    grads = lax.psum(grads, both)
    return (discharge, grads[:feat], grads[feat + steps], grads[feat : feat + steps].T)


def solution(mesh):
    placed = (
        P(("section", "tile"), None),
        P(),
        P(),
        P(),
        P(("section", "tile"), None),
        P(("section", "tile")),
        P(None, ("section", "tile")),
        P(None, ("section", "tile")),
        P(None, ("section", "tile")),
        P(None, ("section", "tile"), None),
    )
    return jax.shard_map(
        local,
        mesh=mesh,
        in_specs=placed,
        out_specs=(P(None, ("section", "tile"), None), P(), P(), P()),
        check_vma=False,
    )
```

```python
import functools

import jax
import jax.numpy as jnp
from jax import lax
from jax.experimental import pallas as pl
from jax.experimental.pallas import tpu as pltpu
from jax.sharding import PartitionSpec as P

F32 = jnp.float32
BF16 = jnp.bfloat16


def coefficients(k_ratio, x_weight):
    storage = 2.0 * k_ratio * (1.0 - x_weight)
    denom = storage + 1.0
    c_now = (1.0 - 2.0 * k_ratio * x_weight) / denom
    c_prev = (1.0 + 2.0 * k_ratio * x_weight) / denom
    c_keep = (storage - 1.0) / denom
    c_side = 2.0 / denom
    return (c_now, c_prev, c_keep, c_side)


def later(x, n):
    t = lax.broadcasted_iota(jnp.int32, x.shape, 0)
    return jnp.where(t >= n, pltpu.roll(x, n, 0), 0.0)


def earlier(x, n):
    t = lax.broadcasted_iota(jnp.int32, x.shape, 0)
    return jnp.where(t < x.shape[0] - n, pltpu.roll(x, x.shape[0] - n, 0), 0.0)


def scan_time(drive, decay, shift):
    n = 1
    while n < drive.shape[0]:
        drive = drive + decay * shift(drive, n)
        decay = decay * decay
        n *= 2
    return drive


def exact_dot(x, table, dims):
    total = None
    for _ in range(3):
        part = x.astype(BF16)
        x = x - part.astype(F32)
        term = lax.dot_general(part, table, (dims, ((), ())), preferred_element_type=F32)
        total = term if total is None else total + term
    return total


def joined(parts):
    return jnp.concatenate(parts, axis=1)


def section_coefs(rows, groups):
    k_ratio = joined([rows[g : g + 1] for g in range(groups)])
    x_weight = joined([rows[groups + g : groups + g + 1] for g in range(groups)])
    return coefficients(k_ratio, x_weight)


def by_link(x, rows, groups, span, dims):
    spots = lax.broadcasted_iota(jnp.int32, (span, span), 0).astype(F32)
    out = []
    for g in range(groups):
        table = (spots == rows[2 * groups + g : 2 * groups + g + 1]).astype(F32).astype(BF16)
        out.append(exact_dot(x[:, g * span : (g + 1) * span], table, dims))
    return joined(out)


def adjoint_chain(rows, cot, groups, sections, span, emit):
    extra = None
    for s in reversed(range(sections)):
        c_now, c_prev, c_keep, c_side = section_coefs(rows(s), groups)
        grad = joined([cot(g, s).T for g in range(groups)])
        if extra is not None:
            grad = grad + extra
        adj = scan_time(grad, c_keep, earlier)
        emit(s, c_side * adj)
        if s > 0:
            grad_in = c_now * adj + c_prev * earlier(adj, 1)
            extra = by_link(grad_in, rows(s - 1), groups, span, ((1,), (0,)))


def forward_chain(rows, lat, groups, sections, span, emit):
    inflow = None
    for s in range(sections):
        own = rows(s)
        c_now, c_prev, c_keep, c_side = section_coefs(own, groups)
        drive = c_side * joined([lat(g, s).T for g in range(groups)])
        if inflow is not None:
            drive = drive + c_now * inflow + c_prev * later(inflow, 1)
        flow = scan_time(drive, c_keep, later)
        emit(s, flow)
        if s + 1 < sections:
            inflow = by_link(flow, own, groups, span, ((1,), (1,)))


def step_kernel(
    groups, sections, tiles, reaches, block,
    x_ref, key_ref, w_in_ref, bias_ref, w_out_ref, own_ref,
    flow_out, w_in_out, bias_out, w_out_out,
    hidden_ref, slope_ref, cot_ref, lat_ref, lat_part, lat_all, glat_ref, grads_ref, bias_acc,
    flow_ref, ws_ref, wr1, wsum, ws2, wr2, wg, br1, br2, bias_sum,
    sec_send, sec_recv, tile_send, tile_recv,
):
    span = tiles * reaches
    slots = groups * reaches
    n_blocks = x_ref.shape[0] // block
    feat, hid = w_in_ref.shape
    steps = w_out_ref.shape[1]
    chunk_rows, chunk_cols = wg.shape[2:]
    col_split = hid // chunk_cols
    sec, tile = lax.axis_index("section"), lax.axis_index("tile")

    barrier = pltpu.get_barrier_semaphore()
    for axis, me, n in (("section", sec, sections), ("tile", tile, tiles)):
        for d in range(1, n):
            pl.semaphore_signal(
                barrier, inc=1, device_id={axis: lax.rem(me + d, n)},
                device_id_type=pl.DeviceIdType.MESH,
            )
    pl.semaphore_wait(barrier, sections + tiles - 2)

    def push(axis, phase, src, dst):
        me, n, send, recv = (
            (sec, sections, sec_send, sec_recv)
            if axis == "section"
            else (tile, tiles, tile_send, tile_recv)
        )
        copies = []
        for d in range(1, n):
            peer = lax.rem(me + d, n)
            copy = pltpu.make_async_remote_copy(
                src_ref=src(peer), dst_ref=dst(d), send_sem=send.at[phase, d],
                recv_sem=recv.at[phase, d], device_id={axis: peer},
                device_id_type=pl.DeviceIdType.MESH,
            )
            copy.start()
            copies.append(copy)
        return copies

    def finish(copies):
        for copy in copies:
            copy.wait()

    cot_ref[sec, tile] = own_ref[...]
    mine = lambda _: cot_ref.at[sec, tile]
    moving = push("tile", 0, mine, mine)

    lat_part[...] = jnp.zeros_like(lat_part)
    grads_ref[...] = jnp.zeros_like(grads_ref)
    bias_acc[...] = jnp.zeros_like(bias_acc)

    def onehot(i):
        rows = lax.broadcasted_iota(jnp.int32, (groups * span, block), 0)
        return (rows == key_ref[i]).astype(F32).astype(BF16)

    def ahead(i, _):
        at = pl.ds(pl.multiple_of(i * block, block), block)
        pre = jnp.dot(x_ref[at, :], w_in_ref[...], preferred_element_type=F32) + bias_ref[...]
        sig = 0.5 * jnp.tanh(0.5 * pre) + 0.5
        act = pre * sig
        slope_ref[at, :] = (sig + act * (1.0 - sig)).astype(BF16)
        hidden = act.astype(BF16)
        hidden_ref[at, :] = hidden
        runoff = (0.125 * jnp.dot(hidden, w_out_ref[...], preferred_element_type=F32)).astype(BF16)
        part = jnp.dot(onehot(i), runoff, preferred_element_type=F32)
        lat_part[...] += part.reshape(lat_part.shape)
        return 0

    def behind(i, _):
        at = pl.ds(pl.multiple_of(i * block, block), block)
        back = jnp.dot(glat_ref[...], onehot(i), preferred_element_type=F32)
        back_t = back.T.astype(BF16)
        grads_ref[feat : feat + steps, :] += jnp.dot(
            back.astype(BF16), hidden_ref[at, :], preferred_element_type=F32
        )
        grad_hidden = lax.dot_general(
            back_t, w_out_ref[...], (((1,), (1,)), ((), ())), preferred_element_type=F32
        )
        grad_pre = grad_hidden * slope_ref[at, :].astype(F32)
        bias_acc[...] += jnp.sum(grad_pre, axis=0, keepdims=True)
        grads_ref[0:feat, :] += jnp.dot(
            x_ref[at, :].T, grad_pre.astype(BF16), preferred_element_type=F32
        )
        return 0

    half = n_blocks // 2
    lax.fori_loop(0, half, ahead, 0)
    finish(moving)
    mine = lambda _: cot_ref.at[sec]
    moving = push("section", 0, mine, mine)
    lax.fori_loop(half, n_blocks, ahead, 0)
    finish(moving)
    moving = push("tile", 1, lambda peer: lat_part.at[:, peer], lambda d: lat_ref.at[d])

    rows = lambda s: cot_ref[s, :, slots:, :].reshape(span, steps).T

    def emit_glat(s, glat):
        @pl.when(sec == s)
        def _():
            glat_ref[...] = (0.125 * glat.astype(BF16).astype(F32)).astype(BF16)

    adjoint_chain(
        rows,
        lambda g, s: cot_ref[s, :, g * reaches : (g + 1) * reaches, :].reshape(span, steps),
        groups, sections, span, emit_glat,
    )

    finish(moving)
    total = lat_part[:, tile]
    for d in range(1, tiles):
        total = total + lat_ref[d]
    lat_all[sec, tile] = total
    mine = lambda _: lat_all.at[sec, tile]
    moving = push("tile", 2, mine, mine)
    lax.fori_loop(0, half, behind, 0)
    finish(moving)
    mine = lambda _: lat_all.at[sec]
    moving = push("section", 1, mine, mine)
    lax.fori_loop(half, n_blocks, behind, 0)
    finish(moving)

    def spot(c):
        r, w = c // col_split * chunk_rows, c % col_split * chunk_cols
        return slice(r, r + chunk_rows), slice(w, w + chunk_cols)

    for s in range(sections):
        for t in range(tiles):
            ws_ref[s, t] = grads_ref[spot(s * tiles + t)].astype(BF16)
    moving = push("section", 2, lambda peer: ws_ref.at[peer], lambda d: wr1.at[d])
    moving += push("section", 3, lambda _: bias_acc, lambda d: br1.at[d])

    def emit_flow(s, flow):
        @pl.when(sec == s)
        def _():
            for g in range(groups):
                flow_ref[g] = flow[:, g * span : (g + 1) * span].T.reshape(tiles, reaches, steps)

    forward_chain(
        rows,
        lambda g, s: lat_all[s, :, g].reshape(span, steps),
        groups, sections, span, emit_flow,
    )
    flow_out[...] = flow_ref[:, tile]

    finish(moving)
    total = ws_ref[sec].astype(F32)
    bias = bias_acc[...]
    for d in range(1, sections):
        total = total + wr1[d].astype(F32)
        bias = bias + br1[d]
    wsum[...] = total
    ws2[...] = total.astype(BF16)
    bias_sum[...] = bias
    moving = push("tile", 3, lambda peer: ws2.at[peer], lambda d: wr2.at[d])
    moving += push("tile", 4, lambda _: bias_sum, lambda d: br2.at[d])
    finish(moving)
    total = wsum[tile]
    for d in range(1, tiles):
        total = total + wr2[d].astype(F32)
        bias = bias + br2[d]
    wg[sec, tile] = total.astype(BF16)
    mine = lambda _: wg.at[sec, tile]
    moving = push("tile", 5, mine, mine)
    bias_out[...] = bias
    finish(moving)
    mine = lambda _: wg.at[sec]
    moving = push("section", 4, mine, mine)
    finish(moving)
    for s in range(sections):
        for t in range(tiles):
            grads_ref[spot(s * tiles + t)] = wg[s, t].astype(F32)
    w_in_out[...] = grads_ref[0:feat, :]
    w_out_out[...] = grads_ref[feat : feat + steps, :].T


def local(
    forcing, w_in, bias_in, w_out, target_tile_index, reach_slot,
    k_ratio, x_weight, down_link, cotangent,
):
    tiles = lax.axis_size("tile")
    sections = lax.axis_size("section")
    cells, feat = forcing.shape
    hid, steps = w_out.shape
    groups, reaches = k_ratio.shape
    span = tiles * reaches
    slots = groups * reaches
    block = min(cells // 2, 512)
    chunks = sections * tiles
    chunk_rows = 8
    chunk_cols = (feat + steps) * hid // (chunks * chunk_rows)

    own = jnp.concatenate([k_ratio, x_weight, down_link.astype(F32)], axis=0).T
    own = jnp.pad(own, ((0, 0), (0, steps - own.shape[1])))
    own = jnp.concatenate([cotangent.reshape(slots, steps), own], axis=0)
    key = (reach_slot // reaches) * span + target_tile_index[:, 0] * reaches + reach_slot % reaches

    vmem = pl.BlockSpec(memory_space=pltpu.VMEM)
    part = (chunk_rows, chunk_cols)
    flow, g_in, g_bias, g_out = pl.pallas_call(
        functools.partial(step_kernel, groups, sections, tiles, reaches, block),
        in_specs=[vmem] * 6,
        out_specs=[vmem] * 4,
        out_shape=[
            jax.ShapeDtypeStruct((groups, reaches, steps), F32),
            jax.ShapeDtypeStruct((feat, hid), F32),
            jax.ShapeDtypeStruct((1, hid), F32),
            jax.ShapeDtypeStruct((hid, steps), F32),
        ],
        scratch_shapes=[
            pltpu.VMEM((cells, hid), BF16),
            pltpu.VMEM((cells, hid), BF16),
            pltpu.VMEM((sections, tiles, slots + reaches, steps), F32),
            pltpu.VMEM((tiles, groups, reaches, steps), F32),
            pltpu.VMEM((groups, tiles, reaches, steps), F32),
            pltpu.VMEM((sections, tiles, groups, reaches, steps), F32),
            pltpu.VMEM((steps, groups * span), BF16),
            pltpu.VMEM((feat + steps, hid), F32),
            pltpu.VMEM((1, hid), F32),
            pltpu.VMEM((groups, tiles, reaches, steps), F32),
            pltpu.VMEM((sections, tiles) + part, BF16),
            pltpu.VMEM((sections, tiles) + part, BF16),
            pltpu.VMEM((tiles,) + part, F32),
            pltpu.VMEM((tiles,) + part, BF16),
            pltpu.VMEM((tiles,) + part, BF16),
            pltpu.VMEM((sections, tiles) + part, BF16),
            pltpu.VMEM((sections, 1, hid), F32),
            pltpu.VMEM((tiles, 1, hid), F32),
            pltpu.VMEM((1, hid), F32),
            pltpu.SemaphoreType.DMA((5, sections)),
            pltpu.SemaphoreType.DMA((5, sections)),
            pltpu.SemaphoreType.DMA((6, tiles)),
            pltpu.SemaphoreType.DMA((6, tiles)),
        ],
        compiler_params=pltpu.CompilerParams(
            vmem_limit_bytes=60 << 20, collective_id=0, has_side_effects=True
        ),
    )(forcing, key.reshape(cells // block, 1, block), w_in, bias_in[None, :], w_out, own)
    return (flow, g_in, g_bias[0], g_out)


def solution(mesh):
    placed = (
        P(("section", "tile"), None),
        P(),
        P(),
        P(),
        P(("section", "tile"), None),
        P(("section", "tile")),
        P(None, ("section", "tile")),
        P(None, ("section", "tile")),
        P(None, ("section", "tile")),
        P(None, ("section", "tile"), None),
    )
    return jax.shard_map(
        local,
        mesh=mesh,
        in_specs=placed,
        out_specs=(P(None, ("section", "tile"), None), P(), P(), P()),
        check_vma=False,
    )
```

```python
import functools

import jax
import jax.numpy as jnp
from jax import lax
from jax.experimental import pallas as pl
from jax.experimental.pallas import tpu as pltpu
from jax.sharding import PartitionSpec as P

F32 = jnp.float32
BF16 = jnp.bfloat16


def coefficients(k_ratio, x_weight):
    storage = 2.0 * k_ratio * (1.0 - x_weight)
    denom = storage + 1.0
    c_now = (1.0 - 2.0 * k_ratio * x_weight) / denom
    c_prev = (1.0 + 2.0 * k_ratio * x_weight) / denom
    c_keep = (storage - 1.0) / denom
    c_side = 2.0 / denom
    return (c_now, c_prev, c_keep, c_side)


def later(x, n):
    t = lax.broadcasted_iota(jnp.int32, x.shape, 0)
    return jnp.where(t >= n, pltpu.roll(x, n, 0), 0.0)


def earlier(x, n):
    t = lax.broadcasted_iota(jnp.int32, x.shape, 0)
    return jnp.where(t < x.shape[0] - n, pltpu.roll(x, x.shape[0] - n, 0), 0.0)


def scan_time(drive, decay, shift):
    n = 1
    while n < drive.shape[0]:
        drive = drive + decay * shift(drive, n)
        decay = decay * decay
        n *= 2
    return drive


def exact_dot(x, table, dims):
    total = None
    for _ in range(3):
        part = x.astype(BF16)
        x = x - part.astype(F32)
        term = lax.dot_general(part, table, (dims, ((), ())), preferred_element_type=F32)
        total = term if total is None else total + term
    return total


def joined(parts):
    return jnp.concatenate(parts, axis=1)


def section_coefs(rows, groups):
    k_ratio = joined([rows[g : g + 1] for g in range(groups)])
    x_weight = joined([rows[groups + g : groups + g + 1] for g in range(groups)])
    return coefficients(k_ratio, x_weight)


def by_link(x, rows, groups, span, dims):
    spots = lax.broadcasted_iota(jnp.int32, (span, span), 0).astype(F32)
    out = []
    for g in range(groups):
        table = (spots == rows[2 * groups + g : 2 * groups + g + 1]).astype(F32).astype(BF16)
        out.append(exact_dot(x[:, g * span : (g + 1) * span], table, dims))
    return joined(out)


def adjoint_chain(rows, cot, groups, sections, span, emit):
    extra = None
    for s in reversed(range(sections)):
        c_now, c_prev, c_keep, c_side = section_coefs(rows(s), groups)
        grad = joined([cot(g, s).T for g in range(groups)])
        if extra is not None:
            grad = grad + extra
        adj = scan_time(grad, c_keep, earlier)
        emit(s, c_side * adj)
        if s > 0:
            grad_in = c_now * adj + c_prev * earlier(adj, 1)
            extra = by_link(grad_in, rows(s - 1), groups, span, ((1,), (0,)))


def forward_chain(rows, lat, groups, sections, span, emit):
    inflow = None
    for s in range(sections):
        own = rows(s)
        c_now, c_prev, c_keep, c_side = section_coefs(own, groups)
        drive = c_side * joined([lat(g, s).T for g in range(groups)])
        if inflow is not None:
            drive = drive + c_now * inflow + c_prev * later(inflow, 1)
        flow = scan_time(drive, c_keep, later)
        emit(s, flow)
        if s + 1 < sections:
            inflow = by_link(flow, own, groups, span, ((1,), (1,)))


def step_kernel(
    groups, sections, tiles, reaches, block,
    x_ref, target_ref, slot_ref, w_in_ref, bias_ref, w_out_ref, k_ref, weight_ref, link_ref, own_ref,
    flow_out, bias_out, wg_out, side_ref,
    hidden_ref, slope_ref, back_ref, cot_ref, lat_ref, lat_part, lat_all, glat_ref, grads_ref,
    bias_acc, flow_ref, ws_ref, wr1, ws2, wr2, wg, br1, br2, bias_sum,
    sec_send, sec_recv, tile_send, tile_recv,
):
    span = tiles * reaches
    slots = groups * reaches
    n_blocks = x_ref.shape[0] // block
    feat, hid = w_in_ref.shape
    steps = w_out_ref.shape[1]
    sec, tile = lax.axis_index("section"), lax.axis_index("tile")
    chips = tiles // 2
    chip, core = tile // 2, lax.rem(tile, 2)

    barrier = pltpu.get_barrier_semaphore()
    for axis, me, n in (("section", sec, sections), ("tile", tile, tiles)):
        for d in range(1, n):
            pl.semaphore_signal(
                barrier, inc=1, device_id={axis: lax.rem(me + d, n)},
                device_id_type=pl.DeviceIdType.MESH,
            )
    pl.semaphore_wait(barrier, sections + tiles - 2)

    def push(way, phase, src, dst):
        n = dict(section=sections, tile=tiles, chip=chips, core=2)[way]
        axis = "section" if way == "section" else "tile"
        send, recv = (sec_send, sec_recv) if way == "section" else (tile_send, tile_recv)
        copies = []
        for d in range(1, n):
            if way == "section":
                peer = lax.rem(sec + d, n)
            elif way == "tile":
                peer = lax.rem(tile + d, n)
            elif way == "chip":
                peer = lax.rem(chip + d, n) * 2 + core
            else:
                peer = chip * 2 + (1 - core)
            copy = pltpu.make_async_remote_copy(
                src_ref=src(peer), dst_ref=dst(d), send_sem=send.at[phase, d],
                recv_sem=recv.at[phase, d], device_id={axis: peer},
                device_id_type=pl.DeviceIdType.MESH,
            )
            copy.start()
            copies.append(copy)
        return copies

    def finish(copies):
        for copy in copies:
            copy.wait()

    side_ref[...] = jnp.zeros_like(side_ref)
    for n, values in enumerate((k_ref[...], weight_ref[...], link_ref[...].astype(F32))):
        side_ref[n * groups : (n + 1) * groups, 0:reaches] = values
    cot_ref[sec, chip, core, 0:slots] = own_ref[...]
    cot_ref[sec, chip, core, slots:] = side_ref[...].T[0:reaches]
    mine = lambda _: cot_ref.at[sec, chip, core]
    moving = push("chip", 6, mine, mine)

    lat_part[...] = jnp.zeros_like(lat_part)
    grads_ref[...] = jnp.zeros_like(grads_ref)
    bias_acc[...] = jnp.zeros_like(bias_acc)

    def onehot(i):
        rows = lax.broadcasted_iota(jnp.int32, (groups * span, block), 0)
        slot = slot_ref[i]
        key = slot + target_ref[i] * reaches
        for g in range(1, groups):
            key = key + jnp.where(slot >= g * reaches, span - reaches, 0)
        return (rows == key).astype(F32).astype(BF16)

    def ahead(i, _):
        at = pl.ds(pl.multiple_of(i * block, block), block)
        pre = jnp.dot(x_ref[at, :], w_in_ref[...], preferred_element_type=F32) + bias_ref[...]
        sig = 0.5 * jnp.tanh(0.5 * pre) + 0.5
        act = pre * sig
        slope_ref[at, :] = (sig + act * (1.0 - sig)).astype(BF16)
        hidden = act.astype(BF16)
        hidden_ref[at, :] = hidden
        runoff = (0.125 * jnp.dot(hidden, w_out_ref[...], preferred_element_type=F32)).astype(BF16)
        part = jnp.dot(onehot(i), runoff, preferred_element_type=F32)
        lat_part[...] += part.reshape(lat_part.shape)
        return 0

    def look(i, _):
        at = pl.ds(pl.multiple_of(i * block, block), block)
        back = jnp.dot(glat_ref[...], onehot(i), preferred_element_type=F32)
        back_ref[at, :] = back.T.astype(BF16)
        grads_ref[0] += jnp.dot(
            back.astype(BF16), hidden_ref[at, :], preferred_element_type=F32
        )
        return 0

    def behind(i, _):
        at = pl.ds(pl.multiple_of(i * block, block), block)
        grad_hidden = lax.dot_general(
            back_ref[at, :], w_out_ref[...], (((1,), (1,)), ((), ())), preferred_element_type=F32
        )
        grad_pre = grad_hidden * slope_ref[at, :].astype(F32)
        bias_acc[...] += jnp.sum(grad_pre, axis=0, keepdims=True)
        grads_ref[1] += jnp.dot(x_ref[at, :].T, grad_pre.astype(BF16), preferred_element_type=F32)
        return 0

    part_of = lambda k: n_blocks * k // 16
    lax.fori_loop(0, part_of(4), ahead, 0)
    finish(moving)
    mine = lambda _: cot_ref.at[sec, :, core]
    moving = push("section", 0, mine, mine)
    lax.fori_loop(part_of(4), part_of(13), ahead, 0)
    finish(moving)
    mine = lambda _: cot_ref.at[:, :, core]
    moving = push("core", 7, mine, mine)
    lax.fori_loop(part_of(13), n_blocks, ahead, 0)
    finish(moving)
    moving = push("tile", 0, lambda peer: lat_part.at[:, peer], lambda d: lat_ref.at[d])

    rows = lambda s: cot_ref[s, :, :, slots:, :].reshape(span, steps).T

    def emit_glat(s, glat):
        @pl.when(sec == s)
        def _():
            glat_ref[...] = (0.125 * glat.astype(BF16).astype(F32)).astype(BF16)

    adjoint_chain(
        rows,
        lambda g, s: cot_ref[s, :, :, g * reaches : (g + 1) * reaches, :].reshape(span, steps),
        groups, sections, span, emit_glat,
    )

    finish(moving)
    total = lat_part[:, tile]
    for d in range(1, tiles):
        total = total + lat_ref[d]
    lat_all[sec, chip, core] = total
    mine = lambda _: lat_all.at[sec, chip, core]
    laterals = push("chip", 8, mine, mine)
    lax.fori_loop(0, part_of(8), look, 0)
    finish(laterals)
    mine_sec = lambda _: lat_all.at[sec, :, core]
    laterals = push("section", 1, mine_sec, mine_sec)
    lax.fori_loop(part_of(8), n_blocks, look, 0)

    def scatter_sections(k, phase):
        for s in range(sections):
            for t in range(tiles):
                ws_ref[k, s, t] = grads_ref[(k,) + spot(wg, hid, s * tiles + t)].astype(BF16)
        return push(
            "section", phase, lambda peer: ws_ref.at[k, peer], lambda d: wr1.at[k, d]
        )

    def scatter_tiles(k, phase):
        total = ws_ref[k, sec].astype(F32)
        for d in range(1, sections):
            total = total + wr1[k, d].astype(F32)
        ws2[k] = total
        return push("tile", phase, lambda peer: ws2.at[k, peer], lambda d: wr2.at[k, d])

    def gather_tiles(k, phase):
        total = ws2[k, tile]
        for d in range(1, tiles):
            total = total + wr2[k, d]
        wg[k, sec, tile] = total.astype(BF16)
        mine = lambda _: wg.at[k, sec, tile]
        return push("tile", phase, mine, mine)

    def gather_sections(k, phase):
        mine = lambda _: wg.at[k, sec]
        return push("section", phase, mine, mine)

    moving = scatter_sections(0, 2)
    lax.fori_loop(0, part_of(5), behind, 0)
    finish(laterals)
    mine_core = lambda _: lat_all.at[:, :, core]
    laterals = push("core", 9, mine_core, mine_core)
    finish(moving)
    moving = scatter_tiles(0, 1)
    lax.fori_loop(part_of(5), part_of(9), behind, 0)
    finish(laterals)
    finish(moving)
    moving = gather_tiles(0, 2)
    lax.fori_loop(part_of(9), part_of(12), behind, 0)
    finish(moving)
    outer = gather_sections(0, 3)
    lax.fori_loop(part_of(12), n_blocks, behind, 0)

    moving = scatter_sections(1, 4)
    moving += push("section", 5, lambda _: bias_acc, lambda d: br1.at[d])

    def emit_flow(s, flow):
        @pl.when(sec == s)
        def _():
            for g in range(groups):
                flow_ref[g] = flow[:, g * span : (g + 1) * span].T.reshape(tiles, reaches, steps)

    forward_chain(
        rows,
        lambda g, s: lat_all[s, :, :, g].reshape(span, steps),
        groups, sections, span, emit_flow,
    )
    flow_out[...] = flow_ref[:, tile]

    finish(outer)
    finish(moving)
    bias = bias_acc[...]
    for d in range(1, sections):
        bias = bias + br1[d]
    bias_sum[...] = bias
    moving = scatter_tiles(1, 3)
    moving += push("tile", 5, lambda _: bias_sum, lambda d: br2.at[d])
    finish(moving)
    moving = gather_tiles(1, 4)
    for d in range(1, tiles):
        bias = bias + br2[d]
    bias_out[...] = bias
    wg_out[0] = wg[0]
    finish(moving)
    moving = gather_sections(1, 6)
    finish(moving)
    wg_out[1] = wg[1]


def spot(chunks, hid, c):
    chunk_rows, chunk_cols = chunks.shape[3:]
    col_split = hid // chunk_cols
    r, w = c // col_split * chunk_rows, c % col_split * chunk_cols
    return slice(r, r + chunk_rows), slice(w, w + chunk_cols)


def unpack_kernel(flow_ref, bias_ref, wg_ref, flow_out, w_in_out, bias_out, w_out_out, turned):
    _, sections, tiles = wg_ref.shape[:3]
    hid = w_in_out.shape[1]
    for s in range(sections):
        for t in range(tiles):
            where = spot(wg_ref, hid, s * tiles + t)
            turned[where] = wg_ref[0, s, t].astype(F32)
            w_in_out[where] = wg_ref[1, s, t].astype(F32)
    w_out_out[...] = turned[...].T
    flow_out[...] = flow_ref[...]
    bias_out[...] = bias_ref[...]


def local(
    forcing, w_in, bias_in, w_out, target_tile_index, reach_slot,
    k_ratio, x_weight, down_link, cotangent,
):
    tiles = lax.axis_size("tile")
    sections = lax.axis_size("section")
    cells, feat = forcing.shape
    hid, steps = w_out.shape
    groups, reaches = k_ratio.shape
    span = tiles * reaches
    slots = groups * reaches
    chips = tiles // 2
    block = min(cells // 2, 512)
    chunk_rows = 8
    chunk_cols = feat * hid // (sections * tiles * chunk_rows)

    vmem = pl.BlockSpec(memory_space=pltpu.VMEM)
    part = (chunk_rows, chunk_cols)
    flow, g_bias, packed = pl.pallas_call(
        functools.partial(step_kernel, groups, sections, tiles, reaches, block),
        in_specs=[vmem] * 10,
        out_specs=[vmem] * 3,
        out_shape=[
            jax.ShapeDtypeStruct((groups, reaches, steps), F32),
            jax.ShapeDtypeStruct((1, hid), F32),
            jax.ShapeDtypeStruct((2, sections, tiles) + part, BF16),
        ],
        scratch_shapes=[
            pltpu.VMEM((steps, steps), F32),
            pltpu.VMEM((cells, hid), BF16),
            pltpu.VMEM((cells, hid), BF16),
            pltpu.VMEM((cells, steps), BF16),
            pltpu.VMEM((sections, chips, 2, slots + reaches, steps), F32),
            pltpu.VMEM((tiles, groups, reaches, steps), F32),
            pltpu.VMEM((groups, tiles, reaches, steps), F32),
            pltpu.VMEM((sections, chips, 2, groups, reaches, steps), F32),
            pltpu.VMEM((steps, groups * span), BF16),
            pltpu.VMEM((2, feat, hid), F32),
            pltpu.VMEM((1, hid), F32),
            pltpu.VMEM((groups, tiles, reaches, steps), F32),
            pltpu.VMEM((2, sections, tiles) + part, BF16),
            pltpu.VMEM((2, sections, tiles) + part, BF16),
            pltpu.VMEM((2, tiles) + part, F32),
            pltpu.VMEM((2, tiles) + part, F32),
            pltpu.VMEM((2, sections, tiles) + part, BF16),
            pltpu.VMEM((sections, 1, hid), F32),
            pltpu.VMEM((tiles, 1, hid), F32),
            pltpu.VMEM((1, hid), F32),
            pltpu.SemaphoreType.DMA((7, sections)),
            pltpu.SemaphoreType.DMA((7, sections)),
            pltpu.SemaphoreType.DMA((10, tiles)),
            pltpu.SemaphoreType.DMA((10, tiles)),
        ],
        compiler_params=pltpu.CompilerParams(
            vmem_limit_bytes=60 << 20, collective_id=0, has_side_effects=True
        ),
    )(
        forcing, target_tile_index.reshape(cells // block, 1, block),
        reach_slot.reshape(cells // block, 1, block), w_in, bias_in[None, :], w_out,
        k_ratio, x_weight, down_link, cotangent.reshape(slots, steps),
    )
    flow, g_in, g_bias, g_out = pl.pallas_call(
        unpack_kernel,
        in_specs=[vmem] * 3,
        out_specs=[vmem] * 4,
        out_shape=[
            jax.ShapeDtypeStruct((groups, reaches, steps), F32),
            jax.ShapeDtypeStruct((feat, hid), F32),
            jax.ShapeDtypeStruct((1, hid), F32),
            jax.ShapeDtypeStruct((hid, steps), F32),
        ],
        scratch_shapes=[pltpu.VMEM((steps, hid), F32)],
    )(flow, g_bias, packed)
    return (flow, g_in, g_bias[0], g_out)


def solution(mesh):
    placed = (
        P(("section", "tile"), None),
        P(),
        P(),
        P(),
        P(("section", "tile"), None),
        P(("section", "tile")),
        P(None, ("section", "tile")),
        P(None, ("section", "tile")),
        P(None, ("section", "tile")),
        P(None, ("section", "tile"), None),
    )
    return jax.shard_map(
        local,
        mesh=mesh,
        in_specs=placed,
        out_specs=(P(None, ("section", "tile"), None), P(), P(), P()),
        check_vma=False,
    )
```

```python
import functools

import jax
import jax.numpy as jnp
from jax import lax
from jax.experimental import pallas as pl
from jax.experimental.pallas import tpu as pltpu
from jax.sharding import PartitionSpec as P

F32 = jnp.float32
BF16 = jnp.bfloat16


def coefficients(k_ratio, x_weight):
    storage = 2.0 * k_ratio * (1.0 - x_weight)
    denom = storage + 1.0
    c_now = (1.0 - 2.0 * k_ratio * x_weight) / denom
    c_prev = (1.0 + 2.0 * k_ratio * x_weight) / denom
    c_keep = (storage - 1.0) / denom
    c_side = 2.0 / denom
    return (c_now, c_prev, c_keep, c_side)


def later(x, n):
    t = lax.broadcasted_iota(jnp.int32, x.shape, 0)
    return jnp.where(t >= n, pltpu.roll(x, n, 0), 0.0)


def earlier(x, n):
    t = lax.broadcasted_iota(jnp.int32, x.shape, 0)
    return jnp.where(t < x.shape[0] - n, pltpu.roll(x, x.shape[0] - n, 0), 0.0)


def scan_time(drive, decay, shift):
    n = 1
    while n < drive.shape[0]:
        drive = drive + decay * shift(drive, n)
        decay = decay * decay
        n *= 2
    return drive


def exact_dot(x, table, dims):
    total = None
    for _ in range(3):
        part = x.astype(BF16)
        x = x - part.astype(F32)
        term = lax.dot_general(part, table, (dims, ((), ())), preferred_element_type=F32)
        total = term if total is None else total + term
    return total


def joined(parts):
    return jnp.concatenate(parts, axis=1)


def section_coefs(rows, groups):
    k_ratio = joined([rows[g : g + 1] for g in range(groups)])
    x_weight = joined([rows[groups + g : groups + g + 1] for g in range(groups)])
    return coefficients(k_ratio, x_weight)


def by_link(x, rows, groups, span, dims):
    spots = lax.broadcasted_iota(jnp.int32, (span, span), 0).astype(F32)
    out = []
    for g in range(groups):
        table = (spots == rows[2 * groups + g : 2 * groups + g + 1]).astype(F32).astype(BF16)
        out.append(exact_dot(x[:, g * span : (g + 1) * span], table, dims))
    return joined(out)


def adjoint_chain(rows, cot, groups, sections, span, emit):
    extra = None
    for s in reversed(range(sections)):
        c_now, c_prev, c_keep, c_side = section_coefs(rows(s), groups)
        grad = joined([cot(g, s).T for g in range(groups)])
        if extra is not None:
            grad = grad + extra
        adj = scan_time(grad, c_keep, earlier)
        emit(s, c_side * adj)
        if s > 0:
            grad_in = c_now * adj + c_prev * earlier(adj, 1)
            extra = by_link(grad_in, rows(s - 1), groups, span, ((1,), (0,)))


def forward_chain(rows, lat, groups, sections, span, emit):
    inflow = None
    for s in range(sections):
        own = rows(s)
        c_now, c_prev, c_keep, c_side = section_coefs(own, groups)
        drive = c_side * joined([lat(g, s).T for g in range(groups)])
        if inflow is not None:
            drive = drive + c_now * inflow + c_prev * later(inflow, 1)
        flow = scan_time(drive, c_keep, later)
        emit(s, flow)
        if s + 1 < sections:
            inflow = by_link(flow, own, groups, span, ((1,), (1,)))


def step_kernel(
    groups, sections, tiles, reaches, block,
    x_ref, target_ref, slot_ref, w_in_ref, bias_ref, w_out_ref, k_ref, weight_ref, link_ref, own_ref,
    flow_out, bias_out, wg_out, side_ref,
    hidden_ref, slope_ref, back_ref, cot_ref, lat_ref, lat_part, lat_all, glat_ref, grads_ref,
    bias_acc, flow_ref, ws_ref, wr1, ws2, wr2, wg, br1, br2, bias_sum,
    sec_send, sec_recv, tile_send, tile_recv,
):
    span = tiles * reaches
    slots = groups * reaches
    n_blocks = x_ref.shape[0] // block
    feat, hid = w_in_ref.shape
    steps = w_out_ref.shape[1]
    sec, tile = lax.axis_index("section"), lax.axis_index("tile")
    chips = tiles // 2
    chip, core = tile // 2, lax.rem(tile, 2)

    barrier = pltpu.get_barrier_semaphore()
    for axis, me, n in (("section", sec, sections), ("tile", tile, tiles)):
        for d in range(1, n):
            pl.semaphore_signal(
                barrier, inc=1, device_id={axis: lax.rem(me + d, n)},
                device_id_type=pl.DeviceIdType.MESH,
            )
    pl.semaphore_wait(barrier, sections + tiles - 2)

    def push(way, phase, src, dst):
        n = dict(section=sections, tile=tiles, chip=chips, core=2)[way]
        axis = "section" if way == "section" else "tile"
        send, recv = (sec_send, sec_recv) if way == "section" else (tile_send, tile_recv)
        copies = []
        for d in range(1, n):
            if way == "section":
                peer = lax.rem(sec + d, n)
            elif way == "tile":
                peer = lax.rem(tile + d, n)
            elif way == "chip":
                peer = lax.rem(chip + d, n) * 2 + core
            else:
                peer = chip * 2 + (1 - core)
            copy = pltpu.make_async_remote_copy(
                src_ref=src(peer), dst_ref=dst(d), send_sem=send.at[phase, d],
                recv_sem=recv.at[phase, d], device_id={axis: peer},
                device_id_type=pl.DeviceIdType.MESH,
            )
            copy.start()
            copies.append(copy)
        return copies

    def finish(copies):
        for copy in copies:
            copy.wait()

    side_ref[...] = jnp.zeros_like(side_ref)
    for n, values in enumerate((k_ref[...], weight_ref[...], link_ref[...].astype(F32))):
        side_ref[n * groups : (n + 1) * groups, 0:reaches] = values
    cot_ref[sec, chip, core, 0:slots] = own_ref[...]
    cot_ref[sec, chip, core, slots:] = side_ref[...].T[0:reaches]
    mine = lambda _: cot_ref.at[sec, chip, core]
    moving = push("chip", 6, mine, mine)

    lat_part[...] = jnp.zeros_like(lat_part)
    grads_ref[...] = jnp.zeros_like(grads_ref)
    bias_acc[...] = jnp.zeros_like(bias_acc)

    def onehot(i):
        rows = lax.broadcasted_iota(jnp.int32, (groups * span, block), 0)
        slot = slot_ref[i]
        key = slot + target_ref[i] * reaches
        for g in range(1, groups):
            key = key + jnp.where(slot >= g * reaches, span - reaches, 0)
        return (rows == key).astype(F32).astype(BF16)

    def ahead(i, _):
        at = pl.ds(pl.multiple_of(i * block, block), block)
        pre = jnp.dot(x_ref[at, :], w_in_ref[...], preferred_element_type=F32) + bias_ref[...]
        sig = 0.5 * jnp.tanh(0.5 * pre) + 0.5
        act = pre * sig
        slope_ref[at, :] = (sig + act * (1.0 - sig)).astype(BF16)
        hidden = act.astype(BF16)
        hidden_ref[at, :] = hidden
        runoff = (0.125 * jnp.dot(hidden, w_out_ref[...], preferred_element_type=F32)).astype(BF16)
        part = jnp.dot(onehot(i), runoff, preferred_element_type=F32)
        lat_part[...] += part.reshape(lat_part.shape)
        return 0

    def look(i, _):
        at = pl.ds(pl.multiple_of(i * block, block), block)
        back = jnp.dot(glat_ref[...], onehot(i), preferred_element_type=F32)
        back_ref[at, :] = back.T.astype(BF16)
        grads_ref[0] += jnp.dot(
            back.astype(BF16), hidden_ref[at, :], preferred_element_type=F32
        )
        return 0

    def behind(i, _):
        at = pl.ds(pl.multiple_of(i * block, block), block)
        grad_hidden = lax.dot_general(
            back_ref[at, :], w_out_ref[...], (((1,), (1,)), ((), ())), preferred_element_type=F32
        )
        grad_pre = grad_hidden * slope_ref[at, :].astype(F32)
        bias_acc[...] += jnp.sum(grad_pre, axis=0, keepdims=True)
        grads_ref[1] += jnp.dot(x_ref[at, :].T, grad_pre.astype(BF16), preferred_element_type=F32)
        return 0

    part_of = lambda k: n_blocks * k // 16
    lax.fori_loop(0, part_of(4), ahead, 0)
    finish(moving)
    mine = lambda _: cot_ref.at[sec, :, core]
    moving = push("section", 0, mine, mine)
    lax.fori_loop(part_of(4), part_of(13), ahead, 0)
    finish(moving)
    mine = lambda _: cot_ref.at[:, :, core]
    moving = push("core", 7, mine, mine)
    lax.fori_loop(part_of(13), n_blocks, ahead, 0)
    finish(moving)
    moving = push("tile", 0, lambda peer: lat_part.at[:, peer], lambda d: lat_ref.at[d])

    rows = lambda s: cot_ref[s, :, :, slots:, :].reshape(span, steps).T

    def emit_glat(s, glat):
        @pl.when(sec == s)
        def _():
            glat_ref[...] = (0.125 * glat.astype(BF16).astype(F32)).astype(BF16)

    adjoint_chain(
        rows,
        lambda g, s: cot_ref[s, :, :, g * reaches : (g + 1) * reaches, :].reshape(span, steps),
        groups, sections, span, emit_glat,
    )

    finish(moving)
    total = lat_part[:, tile]
    for d in range(1, tiles):
        total = total + lat_ref[d]
    lat_all[sec, chip, core] = total
    mine = lambda _: lat_all.at[sec, chip, core]
    laterals = push("chip", 8, mine, mine)
    lax.fori_loop(0, part_of(8), look, 0)
    finish(laterals)
    mine_sec = lambda _: lat_all.at[sec, :, core]
    laterals = push("section", 1, mine_sec, mine_sec)
    lax.fori_loop(part_of(8), n_blocks, look, 0)

    def scatter_sections(k, phase):
        for s in range(sections):
            for t in range(tiles):
                ws_ref[k, s, t] = grads_ref[(k,) + spot(wg, hid, s * tiles + t)].astype(BF16)
        return push(
            "section", phase, lambda peer: ws_ref.at[k, peer], lambda d: wr1.at[k, d]
        )

    def scatter_tiles(k, phase):
        total = ws_ref[k, sec].astype(F32)
        for d in range(1, sections):
            total = total + wr1[k, d].astype(F32)
        ws2[k] = total
        return push("tile", phase, lambda peer: ws2.at[k, peer], lambda d: wr2.at[k, d])

    def gather_tiles(k, phase):
        total = ws2[k, tile]
        for d in range(1, tiles):
            total = total + wr2[k, d]
        wg[k, sec, tile] = total.astype(BF16)
        mine = lambda _: wg.at[k, sec, tile]
        return push("tile", phase, mine, mine)

    def gather_sections(k, phase):
        mine = lambda _: wg.at[k, sec]
        return push("section", phase, mine, mine)

    moving = scatter_sections(0, 2)
    lax.fori_loop(0, part_of(5), behind, 0)
    finish(laterals)
    mine_core = lambda _: lat_all.at[:, :, core]
    laterals = push("core", 9, mine_core, mine_core)
    finish(moving)
    moving = scatter_tiles(0, 1)
    lax.fori_loop(part_of(5), part_of(9), behind, 0)
    finish(laterals)
    finish(moving)
    moving = gather_tiles(0, 2)
    lax.fori_loop(part_of(9), part_of(12), behind, 0)
    finish(moving)
    outer = gather_sections(0, 3)
    lax.fori_loop(part_of(12), n_blocks, behind, 0)

    moving = scatter_sections(1, 4)
    moving += push("section", 5, lambda _: bias_acc, lambda d: br1.at[d])

    def emit_flow(s, flow):
        @pl.when(sec == s)
        def _():
            for g in range(groups):
                flow_ref[g] = flow[:, g * span : (g + 1) * span].T.reshape(tiles, reaches, steps)

    forward_chain(
        rows,
        lambda g, s: lat_all[s, :, :, g].reshape(span, steps),
        groups, sections, span, emit_flow,
    )
    flow_out[...] = flow_ref[:, tile]

    finish(outer)
    finish(moving)
    bias = bias_acc[...]
    for d in range(1, sections):
        bias = bias + br1[d]
    bias_sum[...] = bias
    moving = scatter_tiles(1, 3)
    moving += push("tile", 5, lambda _: bias_sum, lambda d: br2.at[d])
    finish(moving)
    moving = gather_tiles(1, 4)
    for d in range(1, tiles):
        bias = bias + br2[d]
    bias_out[...] = bias
    wg_out[0] = wg[0]
    finish(moving)
    moving = gather_sections(1, 6)
    finish(moving)
    wg_out[1] = wg[1]


def spot(chunks, hid, c):
    chunk_rows, chunk_cols = chunks.shape[3:]
    col_split = hid // chunk_cols
    r, w = c // col_split * chunk_rows, c % col_split * chunk_cols
    return slice(r, r + chunk_rows), slice(w, w + chunk_cols)


def unpack_kernel(flow_ref, bias_ref, wg_ref, flow_out, w_in_out, bias_out, w_out_out, turned):
    _, sections, tiles = wg_ref.shape[:3]
    hid = w_in_out.shape[1]
    for s in range(sections):
        for t in range(tiles):
            where = spot(wg_ref, hid, s * tiles + t)
            turned[where] = wg_ref[0, s, t].astype(F32)
            w_in_out[where] = wg_ref[1, s, t].astype(F32)
    w_out_out[...] = turned[...].T
    flow_out[...] = flow_ref[...]
    bias_out[...] = bias_ref[...]


def local(
    forcing, w_in, bias_in, w_out, target_tile_index, reach_slot,
    k_ratio, x_weight, down_link, cotangent,
):
    tiles = lax.axis_size("tile")
    sections = lax.axis_size("section")
    cells, feat = forcing.shape
    hid, steps = w_out.shape
    groups, reaches = k_ratio.shape
    span = tiles * reaches
    slots = groups * reaches
    chips = tiles // 2
    block = min(cells // 2, 1024 if groups * span <= 512 else 512)
    chunk_rows = 8
    chunk_cols = feat * hid // (sections * tiles * chunk_rows)

    vmem = pl.BlockSpec(memory_space=pltpu.VMEM)
    part = (chunk_rows, chunk_cols)
    flow, g_bias, packed = pl.pallas_call(
        functools.partial(step_kernel, groups, sections, tiles, reaches, block),
        in_specs=[vmem] * 10,
        out_specs=[vmem] * 3,
        out_shape=[
            jax.ShapeDtypeStruct((groups, reaches, steps), F32),
            jax.ShapeDtypeStruct((1, hid), F32),
            jax.ShapeDtypeStruct((2, sections, tiles) + part, BF16),
        ],
        scratch_shapes=[
            pltpu.VMEM((steps, steps), F32),
            pltpu.VMEM((cells, hid), BF16),
            pltpu.VMEM((cells, hid), BF16),
            pltpu.VMEM((cells, steps), BF16),
            pltpu.VMEM((sections, chips, 2, slots + reaches, steps), F32),
            pltpu.VMEM((tiles, groups, reaches, steps), F32),
            pltpu.VMEM((groups, tiles, reaches, steps), F32),
            pltpu.VMEM((sections, chips, 2, groups, reaches, steps), F32),
            pltpu.VMEM((steps, groups * span), BF16),
            pltpu.VMEM((2, feat, hid), F32),
            pltpu.VMEM((1, hid), F32),
            pltpu.VMEM((groups, tiles, reaches, steps), F32),
            pltpu.VMEM((2, sections, tiles) + part, BF16),
            pltpu.VMEM((2, sections, tiles) + part, BF16),
            pltpu.VMEM((2, tiles) + part, F32),
            pltpu.VMEM((2, tiles) + part, F32),
            pltpu.VMEM((2, sections, tiles) + part, BF16),
            pltpu.VMEM((sections, 1, hid), F32),
            pltpu.VMEM((tiles, 1, hid), F32),
            pltpu.VMEM((1, hid), F32),
            pltpu.SemaphoreType.DMA((7, sections)),
            pltpu.SemaphoreType.DMA((7, sections)),
            pltpu.SemaphoreType.DMA((10, tiles)),
            pltpu.SemaphoreType.DMA((10, tiles)),
        ],
        compiler_params=pltpu.CompilerParams(
            vmem_limit_bytes=60 << 20, collective_id=0, has_side_effects=True
        ),
    )(
        forcing, target_tile_index.reshape(cells // block, 1, block),
        reach_slot.reshape(cells // block, 1, block), w_in, bias_in[None, :], w_out,
        k_ratio, x_weight, down_link, cotangent.reshape(slots, steps),
    )
    flow, g_in, g_bias, g_out = pl.pallas_call(
        unpack_kernel,
        in_specs=[vmem] * 3,
        out_specs=[vmem] * 4,
        out_shape=[
            jax.ShapeDtypeStruct((groups, reaches, steps), F32),
            jax.ShapeDtypeStruct((feat, hid), F32),
            jax.ShapeDtypeStruct((1, hid), F32),
            jax.ShapeDtypeStruct((hid, steps), F32),
        ],
        scratch_shapes=[pltpu.VMEM((steps, hid), F32)],
    )(flow, g_bias, packed)
    return (flow, g_in, g_bias[0], g_out)


def solution(mesh):
    placed = (
        P(("section", "tile"), None),
        P(),
        P(),
        P(),
        P(("section", "tile"), None),
        P(("section", "tile")),
        P(None, ("section", "tile")),
        P(None, ("section", "tile")),
        P(None, ("section", "tile")),
        P(None, ("section", "tile"), None),
    )
    return jax.shard_map(
        local,
        mesh=mesh,
        in_specs=placed,
        out_specs=(P(None, ("section", "tile"), None), P(), P(), P()),
        check_vma=False,
    )
```
